256 devices in a mesh: slab: 64 (over y, z, core), grp: 4 (over x).
Axes of the slice: x: 4, y: 4, z: 8, core: 2. Of those that a mesh axis runs over, the one named last changes fastest.
Arguments:
- blocks: bfloat16 [4, 4, 1024, 128, 128], P('grp', None, 'slab'), may hold values from -6 to 6
- coords: int32 [4, 64, 4, 2], P('grp', 'slab'), may hold values from 0 to 15
- counts: int32 [4, 64], P('grp', 'slab'), may hold values from 1 to 4, as said below
- omega1: bfloat16 [1024, 512], replicated, may hold values from -0.1875 to 0.1875
- omega2: bfloat16 [2048, 512], replicated, may hold values from -0.5 to 0.5
- omega3: bfloat16 [2048, 512], replicated, may hold values from -0.125 to 0.125
Outputs:
- core_sketch: float32 [512, 512, 512], P(None, 'slab', 'grp')
The draws below stay inside these ranges and needn't reach their ends.
Inputs may be any that keep to these rules, and one draw needn't show every extreme that they name: counts[g, s] slots are live in the list of group g on slab s; slots from it on are ignored. Some list holds 4 live slots in every draw.
All inputs are finite; a program needn't handle non-finite values.
Results may differ from the reference program's by a relative error of at most 0.0041.
Values may be sent and summed in bfloat16 or wider, within the bound.
No kernel may reach another device: no remote copies, remote signals or barrier semaphores. Data moves between devices by JAX's collectives and lax.ppermute only.
A program may use at most 128 MiB of HBM per device.

```python
import jax
import jax.numpy as jnp
from jax import lax

RANK = 512
BLK = 128
ROWS_DEV = 16
MAX_BLOCKS = 4
NBLK = 16
ROWS = 1024
N_SLAB = 64
N_GRP = 4


def draw_counts(key, part):
    key_heavy = jax.random.fold_in(key, 11)
    key_big = jax.random.fold_in(key, 12)
    key_small = jax.random.fold_in(key, 13)
    key_top = jax.random.fold_in(key, 14)
    heavy = jax.random.randint(key_heavy, (N_SLAB,), 0, N_GRP)
    bigger = jax.random.randint(key_big, (N_SLAB,), MAX_BLOCKS // 2, MAX_BLOCKS + 1)
    smaller = jax.random.randint(key_small, (N_GRP, N_SLAB), 1, MAX_BLOCKS // 4 + 1)
    group_ids = jnp.arange(N_GRP)[:, None]
    slab_ids = jnp.arange(N_SLAB)[None, :]
    is_heavy = group_ids == heavy[None, :]
    counts = jnp.where(is_heavy, bigger[None, :], smaller)
    top_slab = jax.random.randint(key_top, (), 0, N_SLAB)
    counts = jnp.where(is_heavy & (slab_ids == top_slab), MAX_BLOCKS, counts)
    return counts.astype(jnp.int32)


def touch_ends(drawn, stream_key, least, top_value):
    longest = drawn.shape.index(max(drawn.shape))
    spots = []
    for shift in (0, 1):
        where = [jax.random.randint(jax.random.fold_in(stream_key, axis), (), 0, length) for axis, length in enumerate(drawn.shape)]
        where[longest] = (where[longest] + shift) % drawn.shape[longest]
        spots.append(tuple(where))
    return drawn.at[spots[0]].set(least).at[spots[1]].set(top_value)


def levels(rng, dims, cuts, least, largest):
    level = 1.0
    for dim, blocks in cuts:
        heights = jax.random.uniform(jax.random.fold_in(jax.random.fold_in(rng, 6), dim), (blocks,), jnp.float32, least / len(cuts), largest / len(cuts))
        level = level * jnp.repeat(jnp.exp(heights), dims[dim] // blocks).reshape((-1,) + (1,) * (len(dims) - 1 - dim))
    return level


def gaussian(own_key, dims, spread, bound, cuts=(), kind=jnp.bfloat16):
    gain = levels(own_key, dims, cuts, -0.22, 0.18) if cuts else 1.0
    values = jax.random.normal(own_key, dims, jnp.float32) * spread * gain
    return jnp.minimum(jnp.maximum(values, -bound), bound).astype(kind)


def setup_inputs(seed: int = 0) -> dict:
    streams_of = jax.random.split(jax.random.key(seed), 7)
    return {
        "blocks": gaussian(streams_of[0], (N_GRP, MAX_BLOCKS, ROWS, BLK, BLK), 1.0, 6.0, ((0, 4), (2, 64))),
        "coords": touch_ends(jax.random.randint(streams_of[1], (N_GRP, N_SLAB, MAX_BLOCKS, 2), 0, NBLK), jax.random.fold_in(streams_of[1], 1), 0, NBLK - 1).astype(jnp.int32),
        "counts": draw_counts(jax.random.fold_in(streams_of[6], 71), 0),
        "omega1": gaussian(streams_of[3], (ROWS, RANK), ROWS ** -0.5, 0.1875),
        "omega2": gaussian(streams_of[4], (NBLK * BLK, RANK), BLK ** -0.5, 0.5),
        "omega3": gaussian(streams_of[5], (NBLK * BLK, RANK), (BLK * 16) ** -0.5, 0.125),
    }


def contract(running, one_block, coordinate, omega2, omega3):
    block_edge = one_block.shape[-1]
    third_rows = lax.dynamic_slice_in_dim(omega3, (coordinate[1] * block_edge).astype(jnp.int32), block_edge, 0)
    second_rows = lax.dynamic_slice_in_dim(omega2, (coordinate[0] * block_edge).astype(jnp.int32), block_edge, 0)
    after_third = jnp.einsum("iab,bs->ias", one_block.astype(jnp.float32), third_rows.astype(jnp.float32)).astype(jnp.bfloat16)
    return running + jnp.einsum("ias,ar->irs", after_third.astype(jnp.float32), second_rows.astype(jnp.float32))


def reference(blocks, coords, counts, omega1, omega2, omega3):
    def slab_sketch(slab_index):
        running = jnp.zeros((ROWS_DEV, RANK, RANK), jnp.float32)
        for group_index in range(N_GRP):
            def add_slot(position, running, group_index=group_index):
                position = position.astype(jnp.int32)
                one_block = lax.dynamic_slice(blocks, (jnp.int32(group_index), position, (slab_index * ROWS_DEV).astype(jnp.int32), jnp.int32(0), jnp.int32(0)), (1, 1, ROWS_DEV, BLK, BLK))[0, 0]
                coordinate = lax.dynamic_slice(coords, (jnp.int32(group_index), slab_index.astype(jnp.int32), position, jnp.int32(0)), (1, 1, 1, 2))[0, 0, 0]
                return contract(running, one_block, coordinate, omega2, omega3)
            running = lax.fori_loop(jnp.int32(0), counts[group_index, slab_index].astype(jnp.int32), add_slot, running)
        return running

    sketch = lax.map(slab_sketch, jnp.arange(N_SLAB, dtype=jnp.int32))
    folded = sketch.reshape(ROWS, RANK, RANK).astype(jnp.bfloat16)
    return jnp.einsum("ir,ipq->rpq", omega1.astype(jnp.float32), folded.astype(jnp.float32))
```

```python
import functools

import jax
import jax.numpy as jnp
from jax import lax
from jax.experimental import pallas as pl
from jax.experimental.pallas import tpu as pltpu
from jax.sharding import PartitionSpec as P

EDGE = 128
CHUNKS = ((0, 4),)


def fold_kernel(slots, meta, *refs):
    pieces, (omega2t, omega3, out, after, second, acc) = refs[:-6], refs[-6:]
    rows, rank = acc.shape[0], acc.shape[2]

    base = 0
    for source, piece in enumerate(pieces):
        live = meta[source, 2 * slots]

        def one_slot(slot, carry, piece=piece, source=source, base=base):
            at = pl.multiple_of((base + slot) * EDGE, EDGE)
            third = pl.multiple_of(meta[source, 2 * slot + 1] * EDGE, EDGE)
            mode2 = pl.multiple_of(meta[source, 2 * slot] * EDGE, EDGE)
            block = piece[slot].reshape(rows * EDGE, EDGE)
            product = jnp.dot(
                block, omega3[pl.ds(third, EDGE), :], preferred_element_type=jnp.float32
            ).astype(jnp.bfloat16)
            for row in range(rows):
                after[row, pl.ds(at, EDGE), :] = product[row * EDGE : (row + 1) * EDGE]
            second[:, pl.ds(at, EDGE)] = omega2t[:, pl.ds(mode2, EDGE)]
            return carry

        lax.fori_loop(0, live, one_slot, 0)
        base = base + live

    pairs = (base + 1) // 2

    @pl.when(base % 2 == 1)
    def _():
        at = pl.multiple_of(base * EDGE, EDGE)
        for row in range(rows):
            after[row, pl.ds(at, EDGE), :] = jnp.zeros((EDGE, rank), jnp.bfloat16)
        second[:, pl.ds(at, EDGE)] = jnp.zeros((rank, EDGE), jnp.bfloat16)

    def add_pair(pair, first):
        at = pl.multiple_of(pair * 2 * EDGE, 2 * EDGE)
        for row in range(rows):
            term = jnp.dot(
                second[:, pl.ds(at, 2 * EDGE)],
                after[row, pl.ds(at, 2 * EDGE), :],
                preferred_element_type=jnp.float32,
            )
            acc[row] = term if first else acc[row] + term

    add_pair(0, True)

    def next_pair(pair, carry):
        add_pair(pair, False)
        return carry

    lax.fori_loop(1, pairs, next_pair, 0)

    groups = out.shape[1]
    width = rank // groups
    for row in range(rows):
        for group in range(groups):
            cols = acc[row, :, group * width : (group + 1) * width]
            out[:, group, row] = cols.reshape(out.shape[0], out.shape[3], width).astype(jnp.bfloat16)


def fold(meta, pieces, omega2t, omega3, slabs, groups):
    slots, rows = pieces[0].shape[:2]
    rank = omega2t.shape[0]
    depth = len(pieces) * slots * EDGE
    vmem = pl.BlockSpec(memory_space=pltpu.VMEM)
    return pl.pallas_call(
        functools.partial(fold_kernel, slots),
        out_shape=jax.ShapeDtypeStruct(
            (slabs, groups, rows, rank // slabs, rank // groups), jnp.bfloat16
        ),
        in_specs=[pl.BlockSpec(memory_space=pltpu.SMEM)] + [vmem] * (len(pieces) + 2),
        out_specs=vmem,
        scratch_shapes=[
            pltpu.VMEM((rows, depth, rank), jnp.bfloat16),
            pltpu.VMEM((rank, depth), jnp.bfloat16),
            pltpu.VMEM((rows, rank, rank), jnp.float32),
        ],
        compiler_params=pltpu.CompilerParams(vmem_limit_bytes=32 << 20),
        cost_estimate=pl.CostEstimate(
            flops=rows * depth * rank * rank, bytes_accessed=8 << 20, transcendentals=0
        ),
        name="fold",
    )(meta, *pieces, omega2t, omega3)


def core_kernel(*refs):
    count = (len(refs) - 2) // 2
    arrived, weights, (out, wide) = refs[:count], refs[count : 2 * count], refs[-2:]
    rank = weights[0].shape[0]
    strip = arrived[0].shape[-2]
    starts = []
    base = 0
    for piece in arrived:
        size = piece.shape[0]
        starts.append(base)
        wide[base * strip : (base + size) * strip] = (
            piece[...].astype(jnp.float32).reshape(size * strip, EDGE)
        )
        base += size
    for second in range(0, strip, 2):
        total = None
        for piece, weight, start in zip(arrived, weights, starts):
            size = piece.shape[0]
            columns = [
                wide[pl.ds(start * strip + second + k, size, stride=strip), :].astype(jnp.bfloat16)
                for k in range(2)
            ]
            term = jnp.dot(
                weight[...],
                jnp.concatenate(columns, axis=1),
                preferred_element_type=jnp.float32,
            )
            total = term if total is None else total + term
        for k in range(2):
            out[pl.ds(second + k, rank, stride=strip), :] = total[:, k * EDGE : (k + 1) * EDGE]


def core(arrived, weights):
    rank = weights[0].shape[0]
    strip = arrived[0].shape[-2]
    rows = sum(piece.shape[0] for piece in arrived)
    vmem = pl.BlockSpec(memory_space=pltpu.VMEM)
    flat = pl.pallas_call(
        core_kernel,
        out_shape=jax.ShapeDtypeStruct((rank * strip, EDGE), jnp.float32),
        in_specs=[vmem] * (2 * len(arrived)),
        out_specs=vmem,
        scratch_shapes=[pltpu.VMEM((rows * strip, EDGE), jnp.float32)],
        compiler_params=pltpu.CompilerParams(vmem_limit_bytes=24 << 20),
        cost_estimate=pl.CostEstimate(
            flops=2 * rows * rank * strip * EDGE, bytes_accessed=4 << 20, transcendentals=0
        ),
        name="core",
    )(*arrived, *weights)
    return flat.reshape(rank, strip, EDGE)


def local(slabs, groups, blocks, coords, counts, omega1, omega2, omega3):
    me = lax.axis_index("grp")
    own = blocks[0]
    slots, depth = own.shape[:2]
    share = depth // groups
    rank = omega2.shape[1]
    facts = jnp.concatenate([coords[0, 0].reshape(-1), counts[0]])

    def shift(value, step):
        if step == 0:
            return value
        return lax.ppermute(value, "grp", [(i, (i + step) % groups) for i in range(groups)])

    meta = jnp.stack([shift(facts, step) for step in range(groups)])
    omega2t = omega2.T
    heads = omega1.T.reshape(rank, slabs * groups, share)
    arrived, weights = [], []
    for start, size in CHUNKS:
        pieces = []
        for step in range(groups):
            row = ((me + step) % groups) * share + start
            piece = lax.dynamic_slice_in_dim(own, row, size, 1)
            pieces.append(shift(piece, step))
        folded = fold(meta, pieces, omega2t, omega3, slabs, groups)
        folded = folded.reshape((slabs * groups,) + folded.shape[2:])
        folded = lax.all_to_all(folded, ("slab", "grp"), 0, 0, tiled=True)
        arrived.append(folded.reshape((-1,) + folded.shape[2:]))
        weights.append(heads[:, :, start : start + size].reshape(rank, -1))
    return core(arrived, weights)


def solution(mesh):
    in_specs = (
        P("grp", None, "slab", None, None),
        P("grp", "slab", None, None),
        P("grp", "slab"),
        P(),
        P(),
        P(),
    )
    out_specs = P(None, "slab", "grp")
    body = functools.partial(local, mesh.shape["slab"], mesh.shape["grp"])
    return jax.shard_map(body, mesh=mesh, in_specs=in_specs, out_specs=out_specs, check_vma=False)
```

```python
import functools

import jax
import jax.numpy as jnp
from jax import lax
from jax.experimental import pallas as pl
from jax.experimental.pallas import tpu as pltpu
from jax.sharding import PartitionSpec as P


EDGE = 128
SIDE_Y, SIDE_Z, CORES = 4, 8, 2
CHUNKS, ROWS = 2, 2
LEAVE = (4, 3, 5, 2, 6, 1, 7)
STAGE_LIMIT = 16 << 20
FOLD_LIMIT = (40 << 20, 56 << 20)
VMEM = pl.BlockSpec(memory_space=pltpu.VMEM)


def stage_kernel(omega, out, sem):
    copy = pltpu.make_async_copy(omega, out, sem)
    copy.start()
    copy.wait()


def stage(omega):
    return pl.pallas_call(
        stage_kernel,
        out_shape=jax.ShapeDtypeStruct(omega.shape, omega.dtype),
        in_specs=[pl.BlockSpec(memory_space=pltpu.HBM)],
        out_specs=VMEM,
        scratch_shapes=[pltpu.SemaphoreType.DMA(())],
        compiler_params=pltpu.CompilerParams(vmem_limit_bytes=STAGE_LIMIT),
        name="stage",
    )(omega)


def fold_kernel(count, meta, *refs):
    outs = refs[-3 - count : -3]
    pieces = refs[: -3 - count]
    pieces, (omega2t, omega3) = pieces[:-2], pieces[-2:]
    after, second, acc = refs[-3:]
    rows, rank = acc.shape[0], acc.shape[2]
    slots = pieces[0].shape[0]
    groups = outs[0].shape[2]
    here = lax.rem(lax.div(lax.axis_index("slab"), CORES), SIDE_Z)

    def place_slot(source, piece, slot, spot):
        third = pl.multiple_of(meta[source, 2 * slot + 1] * EDGE, EDGE)
        mode2 = pl.multiple_of(meta[source, 2 * slot] * EDGE, EDGE)
        at = pl.multiple_of(spot * EDGE, EDGE)
        product = jnp.dot(
            piece[slot].reshape(rows * EDGE, EDGE),
            omega3[pl.ds(third, EDGE), :],
            preferred_element_type=jnp.float32,
        ).astype(jnp.bfloat16)
        for row in range(rows):
            after[row, pl.ds(at, EDGE), :] = product[row * EDGE : (row + 1) * EDGE]
        second[:, pl.ds(at, EDGE)] = omega2t[:, pl.ds(mode2, EDGE)]

    sources = list(enumerate(pieces))
    lists = len(sources)
    base = lists
    for order, (source, piece) in enumerate(sources):
        place_slot(source, piece, 0, order)

        def one_slot(slot, carry, source=source, piece=piece, base=base):
            place_slot(source, piece, slot, base + slot - 1)
            return carry

        lax.fori_loop(1, meta[source, 2 * slots], one_slot, 0)
        base = base + meta[source, 2 * slots] - 1

    @pl.when(base % 2 == 1)
    def _():
        at = pl.multiple_of(base * EDGE, EDGE)
        for row in range(rows):
            after[row, pl.ds(at, EDGE), :] = jnp.zeros((EDGE, rank), jnp.bfloat16)
        second[:, pl.ds(at, EDGE)] = jnp.zeros((rank, EDGE), jnp.bfloat16)

    width = rank // groups
    strip = outs[0].shape[4]
    for row in range(rows):
        acc[row] = jnp.dot(
            second[:, : lists * EDGE],
            after[row, : lists * EDGE, :],
            preferred_element_type=jnp.float32,
        )

        def next_pair(pair, carry, row=row):
            at = pl.multiple_of(pair * 2 * EDGE, 2 * EDGE)
            acc[row] += jnp.dot(
                second[:, pl.ds(at, 2 * EDGE)],
                after[row, pl.ds(at, 2 * EDGE), :],
                preferred_element_type=jnp.float32,
            )
            return carry

        lax.fori_loop(lists // 2, (base + 1) // 2, next_pair, 0)
        for step in range(SIDE_Z):
            out, line = (outs[0], step * rows + row) if count == 1 else (outs[step], row)
            there = lax.rem(here + step, SIDE_Z)
            for y in range(SIDE_Y):
                at = pl.multiple_of((y * SIDE_Z + there) * CORES * strip, CORES * strip)
                for group in range(groups):
                    cols = acc[row, pl.ds(at, CORES * strip), group * width : (group + 1) * width]
                    out[y, :, group, line] = cols.reshape(CORES, strip, width).astype(jnp.bfloat16)


def fold(meta, pieces, omega2t, omega3, limit, count, slabs, groups):
    slots, rows = pieces[0].shape[:2]
    rank = omega2t.shape[0]
    depth = groups * slots * EDGE
    form = (SIDE_Y, CORES, groups, rows * SIDE_Z // count, rank // slabs, rank // groups)
    return pl.pallas_call(
        functools.partial(fold_kernel, count),
        out_shape=(jax.ShapeDtypeStruct(form, jnp.bfloat16),) * count,
        in_specs=[pl.BlockSpec(memory_space=pltpu.SMEM)] + [VMEM] * (len(pieces) + 2),
        out_specs=(VMEM,) * count,
        scratch_shapes=[
            pltpu.VMEM((rows, depth, rank), jnp.bfloat16),
            pltpu.VMEM((rank, depth), jnp.bfloat16),
            pltpu.VMEM((rows, rank, rank), jnp.float32),
        ],
        compiler_params=pltpu.CompilerParams(vmem_limit_bytes=limit),
        cost_estimate=pl.CostEstimate(
            flops=rows * depth * rank * rank, bytes_accessed=8 << 20, transcendentals=0
        ),
        name="fold",
    )(meta, *pieces, omega2t, omega3)


def weigh_kernel(omega1, out, rows, sems):
    here = lax.rem(lax.div(lax.axis_index("slab"), CORES), SIDE_Z)
    copies = []
    for chunk in range(CHUNKS):
        for step in range(SIDE_Z):
            there = lax.rem(here - step + SIDE_Z, SIDE_Z)
            copies.append(
                pltpu.make_async_copy(
                    omega1.at[:, there, :, chunk], rows.at[chunk, step], sems.at[chunk, step]
                )
            )
            copies[-1].start()
    for copy in copies:
        copy.wait()
    out[...] = rows[...].reshape(-1, rows.shape[-1]).T


def weigh(omega1):
    height, rank = omega1.shape
    lines = height // (SIDE_Y * SIDE_Z * CORES * CHUNKS)
    return pl.pallas_call(
        weigh_kernel,
        out_shape=jax.ShapeDtypeStruct((rank, height), omega1.dtype),
        in_specs=[pl.BlockSpec(memory_space=pltpu.HBM)],
        out_specs=VMEM,
        scratch_shapes=[
            pltpu.VMEM((CHUNKS, SIDE_Z, SIDE_Y, CORES, lines, rank), omega1.dtype),
            pltpu.SemaphoreType.DMA((CHUNKS, SIDE_Z)),
        ],
        compiler_params=pltpu.CompilerParams(vmem_limit_bytes=STAGE_LIMIT),
        name="weigh",
    )(omega1.reshape(SIDE_Y, SIDE_Z, CORES, CHUNKS, lines, rank))


def join_kernel(*refs):
    rows = refs[0].shape[1]
    for number, piece in enumerate(refs[:-1]):
        refs[-1][:, number * rows : (number + 1) * rows] = piece[...]


def join(pieces):
    height, rows = pieces[0].shape[:2]
    form = (height, rows * len(pieces)) + pieces[0].shape[2:]
    return pl.pallas_call(
        join_kernel,
        out_shape=jax.ShapeDtypeStruct(form, pieces[0].dtype),
        in_specs=[VMEM] * len(pieces),
        out_specs=VMEM,
        compiler_params=pltpu.CompilerParams(vmem_limit_bytes=STAGE_LIMIT),
        name="join",
    )(*pieces)


def split_kernel(whole, *pieces):
    rows = pieces[0].shape[1]
    for number, piece in enumerate(pieces):
        piece[...] = whole[:, number * rows : (number + 1) * rows]


def split(whole, count):
    form = (whole.shape[0], whole.shape[1] // count) + whole.shape[2:]
    return pl.pallas_call(
        split_kernel,
        out_shape=(jax.ShapeDtypeStruct(form, whole.dtype),) * count,
        in_specs=[VMEM],
        out_specs=(VMEM,) * count,
        compiler_params=pltpu.CompilerParams(vmem_limit_bytes=STAGE_LIMIT),
        name="split",
    )(whole)


def core_kernel(chunk, plan, has_sum, *refs):
    arrived, refs = refs[: len(plan)], refs[len(plan) :]
    weights, before = refs[0], refs[1] if has_sum else None
    out, wide = refs[-2:]
    rank = weights.shape[0]
    strip = arrived[0].shape[-2]
    depth = wide.shape[0] // strip
    for steps, piece in zip(plan, arrived):
        size = piece.shape[0] * ROWS
        for order, step in enumerate(steps):
            start = step * size * strip
            part = piece[:, order * ROWS : (order + 1) * ROWS]
            wide[start : start + size * strip] = part.astype(jnp.float32).reshape(
                size * strip, EDGE
            )
    for second in range(0, strip, 2):
        columns = [
            wide[pl.ds(second + k, depth, stride=strip), :].astype(jnp.bfloat16) for k in range(2)
        ]
        total = jnp.dot(
            weights[:, chunk * depth : (chunk + 1) * depth],
            jnp.concatenate(columns, axis=1),
            preferred_element_type=jnp.float32,
        )
        for k in range(2):
            rows = pl.ds(second + k, rank, stride=strip)
            term = total[:, k * EDGE : (k + 1) * EDGE]
            out[rows, :] = term + before[rows, :] if has_sum else term


def core(chunk, plan, arrived, weights, before=None):
    rank, depth = weights.shape
    strip = arrived[0].shape[-2]
    has_sum = before is not None
    return pl.pallas_call(
        functools.partial(core_kernel, chunk, plan, has_sum),
        out_shape=jax.ShapeDtypeStruct((rank * strip, EDGE), jnp.float32),
        in_specs=[VMEM] * (len(arrived) + 1 + has_sum),
        out_specs=VMEM,
        scratch_shapes=[pltpu.VMEM((depth // CHUNKS * strip, EDGE), jnp.float32)],
        compiler_params=pltpu.CompilerParams(vmem_limit_bytes=24 << 20),
        cost_estimate=pl.CostEstimate(
            flops=2 * depth // CHUNKS * rank * strip * EDGE,
            bytes_accessed=4 << 20,
            transcendentals=0,
        ),
        name="core",
    )(*arrived, weights, *([before] if has_sum else []))


def along_z(step):
    def slab(y, z, core):
        return (y * SIDE_Z + z) * CORES + core

    return [
        (slab(y, z, core), slab(y, (z + step) % SIDE_Z, core))
        for y in range(SIDE_Y)
        for z in range(SIDE_Z)
        for core in range(CORES)
    ]


def planes(groups):
    return [
        [
            ((y * SIDE_Z + z) * CORES + core) * groups + group
            for y in range(SIDE_Y)
            for core in range(CORES)
            for group in range(groups)
        ]
        for z in range(SIDE_Z)
    ]


def local(slabs, groups, blocks, coords, counts, omega1, omega2, omega3):
    me = lax.axis_index("grp")
    own = blocks[0]
    facts = jnp.concatenate([coords[0, 0].reshape(-1), counts[0]])

    def shift(value, step):
        return lax.ppermute(value, "grp", [(i, (i + step) % groups) for i in range(groups)])

    pieces = []
    for chunk in range(CHUNKS):
        pieces.append([])
        for step in range(groups):
            row = (chunk * groups + lax.rem(me + step, groups)) * ROWS
            piece = lax.dynamic_slice_in_dim(own, row, ROWS, 1)
            pieces[chunk].append(shift(piece, step) if step else piece)
    meta = jnp.stack([facts] + [shift(facts, step) for step in range(1, groups)])
    omega2t = omega2.T

    def leave(value, step):
        return lax.ppermute(value, "slab", along_z(step))

    def spread(value):
        return lax.all_to_all(
            value, ("slab", "grp"), 0, 0, axis_index_groups=planes(groups), tiled=True
        )

    def flat(value):
        return value.reshape((-1,) + value.shape[3:])

    (last,) = fold(meta, pieces[0], omega2t, stage(omega3), FOLD_LIMIT[0], 1, slabs, groups)
    last = spread(flat(last))
    first = fold(meta, pieces[1], omega2t, omega3, FOLD_LIMIT[1], SIDE_Z, slabs, groups)
    first = [flat(part) for part in first]
    for step in LEAVE:
        first[step] = leave(first[step], step)
    last = list(split(last, SIDE_Z))
    for step in LEAVE:
        last[step] = leave(last[step], step)
    first = join(first)
    first = spread(first)
    weights = weigh(omega1)
    plan = tuple((step,) for step in range(SIDE_Z))
    flat_core = core(0, plan, last, weights)
    flat_core = core(1, (tuple(range(SIDE_Z)),), [first], weights, flat_core)
    return flat_core.reshape(omega1.shape[1], -1, EDGE)


def solution(mesh):
    in_specs = (
        P("grp", None, "slab", None, None),
        P("grp", "slab", None, None),
        P("grp", "slab"),
        P(),
        P(),
        P(),
    )
    out_specs = P(None, "slab", "grp")
    slabs, groups = mesh.shape["slab"], mesh.shape["grp"]

    def body(*args):
        return local(slabs, groups, *args)

    return jax.shard_map(body, mesh=mesh, in_specs=in_specs, out_specs=out_specs, check_vma=False)
```

```python
import functools

import jax
import jax.numpy as jnp
from jax import lax
from jax.experimental import pallas as pl
from jax.experimental.pallas import tpu as pltpu
from jax.sharding import PartitionSpec as P


EDGE = 128
SIDE_Y, SIDE_Z, CORES = 4, 8, 2
CHUNKS, ROWS = 2, 2
LEAVE = (1, 7, 3, 5, 4, 2, 6)
STAGE_LIMIT = 16 << 20
FOLD_LIMIT = (40 << 20, 56 << 20)
VMEM = pl.BlockSpec(memory_space=pltpu.VMEM)


def stage_kernel(omega, out, sem):
    copy = pltpu.make_async_copy(omega, out, sem)
    copy.start()
    copy.wait()


def stage(omega):
    return pl.pallas_call(
        stage_kernel,
        out_shape=jax.ShapeDtypeStruct(omega.shape, omega.dtype),
        in_specs=[pl.BlockSpec(memory_space=pltpu.HBM)],
        out_specs=VMEM,
        scratch_shapes=[pltpu.SemaphoreType.DMA(())],
        compiler_params=pltpu.CompilerParams(vmem_limit_bytes=STAGE_LIMIT),
        name="stage",
    )(omega)


def fold_kernel(count, meta, *refs):
    outs = refs[-3 - count : -3]
    pieces = refs[: -3 - count]
    pieces, (omega2t, omega3) = pieces[:-2], pieces[-2:]
    after, second, acc = refs[-3:]
    rows, rank = acc.shape[0], acc.shape[2]
    slots = pieces[0].shape[0]
    groups = outs[0].shape[2]
    here = lax.rem(lax.div(lax.axis_index("slab"), CORES), SIDE_Z)

    def place_slot(source, piece, slot, spot):
        third = pl.multiple_of(meta[source, 2 * slot + 1] * EDGE, EDGE)
        mode2 = pl.multiple_of(meta[source, 2 * slot] * EDGE, EDGE)
        at = pl.multiple_of(spot * EDGE, EDGE)
        product = jnp.dot(
            piece[slot].reshape(rows * EDGE, EDGE),
            omega3[pl.ds(third, EDGE), :],
            preferred_element_type=jnp.float32,
        ).astype(jnp.bfloat16)
        for row in range(rows):
            after[row, pl.ds(at, EDGE), :] = product[row * EDGE : (row + 1) * EDGE]
        second[:, pl.ds(at, EDGE)] = omega2t[:, pl.ds(mode2, EDGE)]

    sources = list(enumerate(pieces))
    lists = len(sources)
    base = lists
    for order, (source, piece) in enumerate(sources):
        place_slot(source, piece, 0, order)

        def one_slot(slot, carry, source=source, piece=piece, base=base):
            place_slot(source, piece, slot, base + slot - 1)
            return carry

        lax.fori_loop(1, meta[source, 2 * slots], one_slot, 0)
        base = base + meta[source, 2 * slots] - 1

    @pl.when(base % 2 == 1)
    def _():
        at = pl.multiple_of(base * EDGE, EDGE)
        for row in range(rows):
            after[row, pl.ds(at, EDGE), :] = jnp.zeros((EDGE, rank), jnp.bfloat16)
        second[:, pl.ds(at, EDGE)] = jnp.zeros((rank, EDGE), jnp.bfloat16)

    width = rank // groups
    strip = outs[0].shape[4]
    for row in range(rows):
        acc[row] = jnp.dot(
            second[:, : lists * EDGE],
            after[row, : lists * EDGE, :],
            preferred_element_type=jnp.float32,
        )

        def next_pair(pair, carry, row=row):
            at = pl.multiple_of(pair * 2 * EDGE, 2 * EDGE)
            acc[row] += jnp.dot(
                second[:, pl.ds(at, 2 * EDGE)],
                after[row, pl.ds(at, 2 * EDGE), :],
                preferred_element_type=jnp.float32,
            )
            return carry

        lax.fori_loop(lists // 2, (base + 1) // 2, next_pair, 0)
        for step in range(SIDE_Z):
            out, line = (outs[0], step * rows + row) if count == 1 else (outs[step], row)
            there = lax.rem(here + step, SIDE_Z)
            for y in range(SIDE_Y):
                at = pl.multiple_of((y * SIDE_Z + there) * CORES * strip, CORES * strip)
                for group in range(groups):
                    cols = acc[row, pl.ds(at, CORES * strip), group * width : (group + 1) * width]
                    out[y, :, group, line] = cols.reshape(CORES, strip, width).astype(jnp.bfloat16)


def fold(meta, pieces, omega2t, omega3, limit, count, slabs, groups):
    slots, rows = pieces[0].shape[:2]
    rank = omega2t.shape[0]
    depth = groups * slots * EDGE
    form = (SIDE_Y, CORES, groups, rows * SIDE_Z // count, rank // slabs, rank // groups)
    return pl.pallas_call(
        functools.partial(fold_kernel, count),
        out_shape=(jax.ShapeDtypeStruct(form, jnp.bfloat16),) * count,
        in_specs=[pl.BlockSpec(memory_space=pltpu.SMEM)] + [VMEM] * (len(pieces) + 2),
        out_specs=(VMEM,) * count,
        scratch_shapes=[
            pltpu.VMEM((rows, depth, rank), jnp.bfloat16),
            pltpu.VMEM((rank, depth), jnp.bfloat16),
            pltpu.VMEM((rows, rank, rank), jnp.float32),
        ],
        compiler_params=pltpu.CompilerParams(vmem_limit_bytes=limit),
        cost_estimate=pl.CostEstimate(
            flops=rows * depth * rank * rank, bytes_accessed=8 << 20, transcendentals=0
        ),
        name="fold",
    )(meta, *pieces, omega2t, omega3)


def weigh_kernel(omega1, out, rows, sems):
    here = lax.rem(lax.div(lax.axis_index("slab"), CORES), SIDE_Z)
    copies = []
    for chunk in range(CHUNKS):
        for step in range(SIDE_Z):
            there = lax.rem(here - step + SIDE_Z, SIDE_Z)
            copies.append(
                pltpu.make_async_copy(
                    omega1.at[:, there, :, chunk], rows.at[chunk, step], sems.at[chunk, step]
                )
            )
            copies[-1].start()
    for copy in copies:
        copy.wait()
    out[...] = rows[...].reshape(-1, rows.shape[-1]).T


def weigh(omega1):
    height, rank = omega1.shape
    lines = height // (SIDE_Y * SIDE_Z * CORES * CHUNKS)
    return pl.pallas_call(
        weigh_kernel,
        out_shape=jax.ShapeDtypeStruct((rank, height), omega1.dtype),
        in_specs=[pl.BlockSpec(memory_space=pltpu.HBM)],
        out_specs=VMEM,
        scratch_shapes=[
            pltpu.VMEM((CHUNKS, SIDE_Z, SIDE_Y, CORES, lines, rank), omega1.dtype),
            pltpu.SemaphoreType.DMA((CHUNKS, SIDE_Z)),
        ],
        compiler_params=pltpu.CompilerParams(vmem_limit_bytes=STAGE_LIMIT),
        name="weigh",
    )(omega1.reshape(SIDE_Y, SIDE_Z, CORES, CHUNKS, lines, rank))


def join_kernel(*refs):
    rows = refs[0].shape[1]
    for number, piece in enumerate(refs[:-1]):
        refs[-1][:, number * rows : (number + 1) * rows] = piece[...]


def join(pieces):
    height, rows = pieces[0].shape[:2]
    form = (height, rows * len(pieces)) + pieces[0].shape[2:]
    return pl.pallas_call(
        join_kernel,
        out_shape=jax.ShapeDtypeStruct(form, pieces[0].dtype),
        in_specs=[VMEM] * len(pieces),
        out_specs=VMEM,
        compiler_params=pltpu.CompilerParams(vmem_limit_bytes=STAGE_LIMIT),
        name="join",
    )(*pieces)


def split_kernel(whole, *pieces):
    rows = pieces[0].shape[1]
    for number, piece in enumerate(pieces):
        piece[...] = whole[:, number * rows : (number + 1) * rows]


def split(whole, count):
    form = (whole.shape[0], whole.shape[1] // count) + whole.shape[2:]
    return pl.pallas_call(
        split_kernel,
        out_shape=(jax.ShapeDtypeStruct(form, whole.dtype),) * count,
        in_specs=[VMEM],
        out_specs=(VMEM,) * count,
        compiler_params=pltpu.CompilerParams(vmem_limit_bytes=STAGE_LIMIT),
        name="split",
    )(whole)


def core_kernel(plan, *refs):
    arrived, (weights, out, wide) = refs[:-3], refs[-3:]
    rank = weights.shape[0]
    depth = weights.shape[1]
    strip = arrived[0].shape[-2]
    for (chunk, steps), piece in zip(plan, arrived):
        size = piece.shape[0] * ROWS
        for order, step in enumerate(steps):
            start = (chunk * SIDE_Z + step) * size * strip
            part = piece[:, order * ROWS : (order + 1) * ROWS]
            wide[start : start + size * strip] = part.astype(jnp.float32).reshape(
                size * strip, EDGE
            )
    for second in range(0, strip, 2):
        columns = [
            wide[pl.ds(second + k, depth, stride=strip), :].astype(jnp.bfloat16) for k in range(2)
        ]
        total = jnp.dot(
            weights[...], jnp.concatenate(columns, axis=1), preferred_element_type=jnp.float32
        )
        for k in range(2):
            out[pl.ds(second + k, rank, stride=strip), :] = total[:, k * EDGE : (k + 1) * EDGE]


def core(plan, arrived, weights):
    rank, depth = weights.shape
    strip = arrived[0].shape[-2]
    flat = pl.pallas_call(
        functools.partial(core_kernel, plan),
        out_shape=jax.ShapeDtypeStruct((rank * strip, EDGE), jnp.float32),
        in_specs=[VMEM] * (len(arrived) + 1),
        out_specs=VMEM,
        scratch_shapes=[pltpu.VMEM((depth * strip, EDGE), jnp.float32)],
        compiler_params=pltpu.CompilerParams(vmem_limit_bytes=24 << 20),
        cost_estimate=pl.CostEstimate(
            flops=2 * depth * rank * strip * EDGE, bytes_accessed=4 << 20, transcendentals=0
        ),
        name="core",
    )(*arrived, weights)
    return flat.reshape(rank, strip, EDGE)


def along_z(step):
    def slab(y, z, core):
        return (y * SIDE_Z + z) * CORES + core

    return [
        (slab(y, z, core), slab(y, (z + step) % SIDE_Z, core))
        for y in range(SIDE_Y)
        for z in range(SIDE_Z)
        for core in range(CORES)
    ]


def planes(groups):
    return [
        [
            ((y * SIDE_Z + z) * CORES + core) * groups + group
            for y in range(SIDE_Y)
            for core in range(CORES)
            for group in range(groups)
        ]
        for z in range(SIDE_Z)
    ]


def local(slabs, groups, blocks, coords, counts, omega1, omega2, omega3):
    me = lax.axis_index("grp")
    own = blocks[0]
    facts = jnp.concatenate([coords[0, 0].reshape(-1), counts[0]])

    def shift(value, step):
        return lax.ppermute(value, "grp", [(i, (i + step) % groups) for i in range(groups)])

    pieces = []
    for chunk in range(CHUNKS):
        pieces.append([])
        for step in range(groups):
            row = (chunk * groups + lax.rem(me + step, groups)) * ROWS
            piece = lax.dynamic_slice_in_dim(own, row, ROWS, 1)
            pieces[chunk].append(shift(piece, step) if step else piece)
    meta = jnp.stack([facts] + [shift(facts, step) for step in range(1, groups)])
    omega2t = omega2.T

    def leave(value, step):
        return lax.ppermute(value, "slab", along_z(step))

    def spread(value):
        return lax.all_to_all(
            value, ("slab", "grp"), 0, 0, axis_index_groups=planes(groups), tiled=True
        )

    def flat(value):
        return value.reshape((-1,) + value.shape[3:])

    (last,) = fold(meta, pieces[0], omega2t, stage(omega3), FOLD_LIMIT[0], 1, slabs, groups)
    last = spread(flat(last))
    first = fold(meta, pieces[1], omega2t, omega3, FOLD_LIMIT[1], SIDE_Z, slabs, groups)
    first = [flat(part) for part in first]
    for step in LEAVE:
        first[step] = leave(first[step], step)
    last = list(split(last, SIDE_Z))
    for step in LEAVE:
        last[step] = leave(last[step], step)
    first = join(first)
    first = spread(first)
    weights = weigh(omega1)
    plan = [(1, tuple(range(SIDE_Z)))] + [(0, (step,)) for step in range(SIDE_Z)]
    return core(tuple(plan), [first] + last, weights)


def solution(mesh):
    in_specs = (
        P("grp", None, "slab", None, None),
        P("grp", "slab", None, None),
        P("grp", "slab"),
        P(),
        P(),
        P(),
    )
    out_specs = P(None, "slab", "grp")
    slabs, groups = mesh.shape["slab"], mesh.shape["grp"]

    def body(*args):
        return local(slabs, groups, *args)

    return jax.shard_map(body, mesh=mesh, in_specs=in_specs, out_specs=out_specs, check_vma=False)
```
